128 devices in a mesh: lat: 8 (over z, core), lon: 16 (over y, x).
Axes of the slice: x: 4, y: 4, z: 4, core: 2. Of those that a mesh axis runs over, the one named last changes fastest.
Arguments:
- control: float32 [254, 64, 1536], P(None, 'lat', 'lon'), may hold values from -6 to 6
- vert_band: float32 [2, 9, 127], replicated, may hold values from -2.5 to 2.5
- lat_length: float32 [254, 8], replicated, may hold values from 3 to 32
- lon_length: float32 [254], replicated, may hold values from 3 to 192
- band_index: int32 [64], replicated, may hold values from 0 to 7
- owner_device: int32 [254, 1], replicated, may hold values from 0 to 127; in each aligned block of 254 rows (0 to 253, 254 to 507, ...) at most 4 rows name the same one
Outputs:
- winds: float32 [254, 64, 1536], P(None, 'lat', 'lon')
- slabs: float32 [512, 64, 1536], P(('lat', 'lon'))
The draws below stay inside these ranges and needn't reach their ends.
Inputs may be any that keep to these rules, and one draw needn't show every extreme that they name: owner_device[s, 0] numbers a device along the joined axes lat+lon; no device owns more than 4 level-variables, one owns exactly 4, and every device owns at least one.
All inputs are finite; a program needn't handle non-finite values.
Results may differ from the reference program's by a relative error of at most 0.0003.
Values sent between devices are 32-bit elements; how exact they have to be, the bound alone decides.
A program may use at most 64 MiB of HBM per device.

```python
import math
import jax
import jax.numpy as jnp
import numpy as np
from jax import lax

NLEV = 127
VB = 4
NBAND = 8
NLAT_GLOBE = 768
NVL = 254
NLAT = 64
NLON = 1536
MOST = 4
DEVICES = 128


def set_ends(result, stream_key, low, largest):
    dims = result.shape
    spot = [jax.random.randint(jax.random.fold_in(stream_key, axis), (), 0, dims[axis]) for axis in range(len(dims))]
    result = result.at[tuple(spot)].set(low)
    longest = dims.index(max(dims))
    spot[longest] = (spot[longest] + 1) % dims[longest]
    return result.at[tuple(spot)].set(largest)


def levels(key, dims, split, low, high):
    def one(dim, blocks):
        heights = jax.random.uniform(jax.random.fold_in(jax.random.fold_in(key, 6), dim), (blocks,), jnp.float32, low / len(split), high / len(split))
        return jnp.repeat(jnp.exp(heights), dims[dim] // blocks).reshape((-1,) + (1,) * (len(dims) - dim - 1))

    level = one(*split[0])
    for cut in split[1:]:
        level = level * one(*cut)
    return level


def assign_block(rng, own, number, rows, number_of, top, reach, lean):
    sequence = jax.random.permutation(rng, number_of)
    heavy_load, usual = load_shares(number_of, rows * top, reach, lean, True), load_shares(number_of, rows * top, reach, lean, False)
    places = jnp.arange(number_of)

    def named(sizes, rotation):
        used = int((sizes > 0).sum())
        fixed = max(1, used // 4)
        moved = fixed + (places - fixed + rotation * (used - fixed)) % max(1, number_of - fixed)
        return jnp.zeros((number_of,), jnp.int32).at[sequence[jnp.where(places < fixed, places, moved)]].set(jnp.asarray(sizes, jnp.int32))

    sizes = jnp.where(number % 4 == 0, named(heavy_load, number // 4), named(usual, number - number // 4 - 1))
    mixed = jax.random.permutation(jax.random.fold_in(own, 3), number_of)
    giver, sink = mixed[0:number_of // 2 * 2:2], mixed[1:number_of // 2 * 2:2]
    slack = jnp.minimum(sizes[giver] - 1, reach - sizes[sink]) // 2
    slack = jnp.where((giver == sequence[0]) | (sink == sequence[0]) | (sizes[sink] == 0), 0, jnp.maximum(slack, 0))
    moved = jax.random.randint(jax.random.fold_in(own, 4), (number_of // 2,), 0, 1 << 20) % (slack + 1)
    sizes = sizes.at[giver].add(-moved).at[sink].add(moved)
    labels = jnp.searchsorted(jnp.cumsum(sizes), jnp.arange(rows * top), side="right").astype(jnp.int32)
    grid = labels.reshape(top, rows).T
    grid = grid[jax.random.permutation(jax.random.fold_in(own, 1), rows)]
    rotation = jax.random.randint(jax.random.fold_in(own, 2), (rows, 1), 0, top)
    return jnp.take_along_axis(grid, (jnp.arange(top)[None, :] + rotation) % top, axis=1)


def load_shares(amount, total, limit, skew, full):
    weights = [(1 << 20) // math.isqrt(grade ** skew) + 1 for grade in range(1, amount + 1)]
    largest = limit if full else min(limit, max(-(-total // amount), total * weights[0] // sum(weights)))
    least = 1 if total - largest >= amount - 1 else 0
    holding, surplus = [largest] + [least] * (amount - 1), total - largest - least * (amount - 1)
    while surplus > 0:
        candidates = [i for i in range(1, amount) if holding[i] < largest] or [i for i in range(1, amount) if holding[i] < limit]
        whole, remaining = sum([weights[i] for i in candidates]), surplus
        for i in candidates:
            more = min(limit - holding[i], max(1, remaining * weights[i] // whole), surplus)
            holding[i] = holding[i] + more
            surplus = surplus - more
    return np.array(holding)


def bell_draw(stream_key, dims, scale, most, pieces=(), kind=jnp.bfloat16):
    loudness = levels(stream_key, dims, pieces, -0.22, 0.18) if pieces else 1.0
    entries = jax.random.normal(stream_key, dims, jnp.float32) * scale * loudness
    return jnp.minimum(jnp.maximum(entries, -most), most).astype(kind)


def setup_inputs(seed: int = 0) -> dict:
    key_of = jax.random.split(jax.random.key(seed), 7)
    control = bell_draw(key_of[0], (NVL, NLAT, NLON), 1.0, 6.0, ((1, 8), (2, 16)), jnp.float32)
    vert_band = bell_draw(key_of[1], (2, 2 * VB + 1, NLEV), 0.3, 2.5, (), jnp.float32)
    lat_length = jnp.clip(jnp.exp(jax.random.uniform(key_of[2], (NVL, NBAND), jnp.float32, math.log(3.0), math.log(32.0))), 3.0, 32.0)
    lon_length = jnp.clip(jnp.exp(jax.random.uniform(key_of[3], (NVL,), jnp.float32, math.log(3.0), math.log(192.0))), 3.0, 192.0)
    band_index = set_ends(jax.random.randint(key_of[4], (NLAT,), 0, NBAND), jax.random.fold_in(key_of[4], 1), 0, NBAND - 1).astype(jnp.int32)
    owner_device_keys = jax.random.split(jax.random.fold_in(key_of[5], 1), NVL // NVL)
    owner_device_turns = jax.random.permutation(jax.random.fold_in(key_of[5], 3), NVL // NVL)
    owner_device = jax.vmap(lambda own, number: assign_block(jax.random.fold_in(key_of[5], 2), own, number, NVL, DEVICES, 1, MOST, 2))(owner_device_keys, owner_device_turns).reshape((NVL, 1))
    return dict(control=control, vert_band=vert_band, lat_length=lat_length, lon_length=lon_length, band_index=band_index, owner_device=owner_device)


def vertical(control, vert_band):
    fields = control.reshape(2, NLEV, NLAT, NLON)
    summed = fields
    for offset in range(2 * VB + 1):
        moved_by = offset - VB
        if moved_by == 0:
            shifted = fields
        elif moved_by > 0:
            shifted = jnp.concatenate([fields[:, moved_by:], jnp.zeros((2, moved_by, NLAT, NLON), jnp.float32)], axis=1)
        else:
            shifted = jnp.concatenate([jnp.zeros((2, -moved_by, NLAT, NLON), jnp.float32), fields[:, :moved_by]], axis=1)
        summed = summed + vert_band[:, offset, :, None, None] * shifted
    return summed.reshape(NVL, NLAT, NLON)

def run_forward(fields, decays, weights):

    def advance(running, inputs):
        column, factor, gain = inputs
        updated = factor[:, None] * running + gain[:, None] * column
        return (updated, updated)
    initial = jnp.zeros((fields.shape[0], fields.shape[2]), jnp.float32)
    _, values = lax.scan(advance, initial, (jnp.moveaxis(fields, 1, 0), decays.T, weights.T))
    return jnp.moveaxis(values, 0, 1)

def slot_sources(owner_device):
    owners = owner_device[:, 0]
    level_ids = jnp.arange(NVL, dtype=jnp.int32)
    sharing = (owners[:, None] == owners[None, :]) & (level_ids[None, :] < level_ids[:, None])
    rank_in = lax.optimization_barrier(jnp.sum(sharing.astype(jnp.int32), axis=1))
    slot_of = owners * MOST + rank_in
    slot_numbers = jnp.arange(DEVICES * MOST, dtype=jnp.int32)
    matches = slot_of[None, :] == slot_numbers[:, None]
    filled = jnp.any(matches, axis=1)
    source = jnp.argmax(matches.astype(jnp.int32), axis=1).astype(jnp.int32)
    return (source, filled)

def reference(control, vert_band, lat_length, lon_length, band_index, owner_device):
    mixed = vertical(control, vert_band)
    lat_decay = jnp.exp(-1.0 / lat_length[:, band_index])
    lat_weight = jnp.sqrt(1.0 - lat_decay * lat_decay)
    northward = run_forward(mixed, lat_decay, lat_weight)
    southward = jnp.flip(run_forward(jnp.flip(northward, 1), jnp.flip(lat_decay, 1), jnp.flip(lat_weight, 1)), 1)
    inverse = 1.0 / lon_length
    lon_decay = jnp.broadcast_to(jnp.exp(-inverse)[:, None], (NVL, NLON))
    lon_weight = jnp.sqrt(1.0 - lon_decay * lon_decay)
    swapped = jnp.swapaxes(southward, 1, 2)
    places = jnp.arange(NLON, dtype=jnp.float32)
    closing = 1.0 / (1.0 - jnp.exp(-NLON * inverse))
    eastward = run_forward(swapped, lon_decay, lon_weight)
    eastward = eastward + jnp.exp(-(places[None, :] + 1.0) * inverse[:, None])[:, :, None] * (eastward[:, -1:, :] * closing[:, None, None])
    westward = jnp.flip(run_forward(jnp.flip(eastward, 1), lon_decay, lon_weight), 1)
    westward = westward + jnp.exp(-(NLON - places[None, :]) * inverse[:, None])[:, :, None] * (westward[:, :1, :] * closing[:, None, None])
    filtered = jnp.swapaxes(westward, 1, 2)
    source, filled = slot_sources(owner_device)
    slabs = jnp.where(filled[:, None, None], jnp.take(filtered, source, axis=0), 0.0)
    padded = jnp.pad(filtered, ((0, 0), (1, 1), (0, 0)))
    d_lat = (padded[:, 2:, :] - padded[:, :-2, :]) * 0.5
    d_lon = (jnp.roll(filtered, -1, axis=2) - jnp.roll(filtered, 1, axis=2)) * 0.5
    latitude_rows = jnp.arange(NLAT, dtype=jnp.float32) + float(NLAT_GLOBE - NLAT)
    latitude = jnp.pi * ((latitude_rows + 0.5) / NLAT_GLOBE - 0.5)
    metric = (1.0 / jnp.maximum(jnp.cos(latitude), 0.2))[None, :, None]
    east_wind = -d_lat[:NLEV] + d_lon[NLEV:] * metric
    north_wind = d_lon[:NLEV] * metric + d_lat[NLEV:]
    winds = jnp.concatenate([east_wind, north_wind], axis=0)
    return (winds, slabs)
```

```python
import math

import jax
import jax.numpy as jnp
from jax import lax
from jax.experimental import pallas as pl
from jax.experimental.pallas import tpu as pltpu
from jax.sharding import PartitionSpec as P

NLAT_GLOBE = 768
MESH = pl.DeviceIdType.MESH
NVL = 254
NLEV = 127
LANES = 128
COLS = 96
ROWS = 8
GROUPS = 32
SLOTS = 4
CHUNKS = 2


def slot_sources(owner_device, devices_all, most_slots):
    owners = owner_device[:, 0]
    level_ids = jnp.arange(owners.shape[0], dtype=jnp.int32)
    sharing = (owners[:, None] == owners[None, :]) & (level_ids[None, :] < level_ids[:, None])
    rank_in = jnp.sum(sharing.astype(jnp.int32), axis=1)
    slot_of = owners * most_slots + rank_in
    slot_numbers = jnp.arange(devices_all * most_slots, dtype=jnp.int32)
    matches = slot_of[None, :] == slot_numbers[:, None]
    return NVL + jnp.sum(jnp.where(matches, level_ids[None, :] - NVL, 0), axis=1)


def iota(shape, dim):
    return lax.broadcasted_iota(jnp.int32, shape, dim)


def spread(column):
    return jnp.broadcast_to(column, (8, LANES))


def columns_kernel(
    source_ref,
    band_ref,
    table_ref,
    control_ref,
    arrived_ref,
    winds_ref,
    control_in,
    padded,
    mixed,
    field,
    final,
    whole,
    slopes,
    lat_inv,
    lon_send,
    lon_recv,
    lon_acc,
    to_partner,
    own_out,
    near_recv,
    chip_send,
    chip_recv,
    in_send,
    in_recv,
    north_end,
    blocks_out,
    in_sem,
    lon_sems,
    near_sems,
    chip_send_sems,
    chip_recv_sems,
    far_sems,
    all_sems,
):
    lat = lax.axis_index("lat")
    lon = lax.axis_index("lon")
    z, core = lat // 2, lat % 2
    y, x = lon // 4, lon % 4
    me = lat * 16 + lon
    partner = (z * 2 + 1 - core, lon)

    barrier = pltpu.get_barrier_semaphore()

    @pl.loop(1, 16)
    def _(i):
        pl.semaphore_signal(
            barrier, inc=1, device_id=(lat, lax.rem(lon + i, 16)), device_id_type=MESH
        )

    @pl.loop(1, 8)
    def _(i):
        pl.semaphore_signal(
            barrier, inc=1, device_id=(lax.rem(lat + i, 8), lon), device_id_type=MESH
        )

    load = pltpu.make_async_copy(control_ref, control_in, in_sem)
    load.start()

    lane = iota((8, LANES), 1)
    lane_f = lane.astype(jnp.float32)

    band_row = jnp.broadcast_to(table_ref[256:257, :], (8, LANES))

    @pl.loop(0, GROUPS)
    def _(g):
        rows = pl.ds(pl.multiple_of(g * 8, 8), 8)
        lengths = table_ref[rows, :]
        chosen = jnp.ones((8, LANES), jnp.float32)
        for b in range(8):
            chosen = jnp.where(band_row == float(b), spread(lengths[:, b : b + 1]), chosen)
        lat_inv[rows, :] = jnp.where(lane < 64, 1.0 / chosen, 0.0)

    zero_tile = jnp.zeros((8, LANES), jnp.float32)

    @pl.loop(0, 2 * 135)
    def _(r):
        padded[r] = zero_tile

    load.wait()

    for v in range(2):

        @pl.loop(0, NLEV)
        def _(k):
            padded[v * 135 + 4 + k, :, 0:COLS] = control_in[v * NLEV + k]

    for v in range(2):

        @pl.loop(0, NLEV)
        def _(k):
            total = padded[v * 135 + 4 + k]
            for o in range(9):
                total = total + band_ref[v, o, k] * padded[v * 135 + k + o]
            mixed[pl.ds(pl.multiple_of((v * NLEV + k) * 8, 8), 8), :] = pltpu.roll(total, 1, 1)

    mixed[NVL * 8 : NVL * 8 + 8, :] = zero_tile
    mixed[NVL * 8 + 8 : NVL * 8 + 16, :] = zero_tile

    lane16 = lane % 16

    def lon_rate(rows):
        return 1.0 / spread(table_ref[rows, 8:9])

    @pl.loop(0, GROUPS)
    def _(g):
        rows = pl.ds(pl.multiple_of(g * 8, 8), 8)
        inv = lon_rate(rows)
        east_factor, west_factor = [], []
        for k in range(7):
            step = 1 << k
            power = jnp.exp(-float(step) * inv)
            east_factor.append(jnp.where(lane >= step, power, 0.0))
            west_factor.append(jnp.where(lane < LANES - step, power, 0.0))
        states = jnp.zeros((8, LANES), jnp.float32)
        for j in range(8):
            values = mixed[pl.ds(g * 64 + j, 8, stride=8), :]
            east, west = values, values
            for k in range(7):
                step = 1 << k
                east = east + east_factor[k] * pltpu.roll(east, step, 1)
                west = west + west_factor[k] * pltpu.roll(west, LANES - step, 1)
            field[pl.ds(pl.multiple_of(g * 64 + j * 8, 8), 8), :] = east + west - values
            states = jnp.where(lane16 == j, spread(east[:, 96:97]), states)
            states = jnp.where(lane16 == 8 + j, spread(west[:, 1:2]), states)
        part = pl.ds(pl.multiple_of((g // 8) * 8, 8), 8)
        lon_send[part, :] = jnp.where(lane // 16 == g % 8, states, lon_send[part, :])

    pl.semaphore_wait(barrier, 22)

    @pl.loop(1, 16)
    def _(i):
        pltpu.make_async_remote_copy(
            src_ref=lon_send,
            dst_ref=lon_recv.at[lon],
            send_sem=lon_sems.at[0],
            recv_sem=lon_sems.at[1],
            device_id=(lat, lax.rem(lon + i, 16)),
            device_id_type=MESH,
        ).start()

    is_east = lane16 < 8
    for t in range(4):
        inv = jnp.zeros((8, LANES), jnp.float32)
        for b in range(8):
            g = t * 8 + b
            inv = jnp.where(lane // 16 == b, lon_rate(pl.ds(g * 8, 8)), inv)
        lon_acc[32 + t * 8 : 40 + t * 8, :] = inv

    fifteen = lon_recv.at[pl.ds(0, 15)]
    pltpu.make_async_copy(fifteen, fifteen, lon_sems.at[1]).wait()

    for t in range(4):
        part = slice(t * 8, t * 8 + 8)
        inv = lon_acc[32 + t * 8 : 40 + t * 8, :]
        total = lon_send[part, :] * jnp.exp(-(96.0 * 15.0) * inv)
        for dq in range(1, 16):
            got = lon_recv[lax.rem(lon + 16 - dq, 16), part, :]
            blocks = jnp.where(is_east, float(dq - 1), float(15 - dq))
            total = total + got * jnp.exp(-96.0 * blocks * inv)
        lon_acc[part, :] = total / (1.0 - jnp.exp(-1536.0 * inv))

    lat_lane = lane
    first_row = lat * 8
    partner_first = (z * 2 + 1 - core) * 8

    def lat_rates(rows):
        return lat_inv[rows, :]

    def total_between(rates, low, high):
        inside = (lat_lane >= low) & (lat_lane < high)
        return jnp.exp(-jnp.sum(jnp.where(inside, rates, 0.0), axis=1, keepdims=True))

    def own_factors(rates):
        own = pltpu.roll(rates, lax.rem(LANES - first_row, LANES), 1)
        decay = jnp.exp(-own)
        return decay, jnp.sqrt(1.0 - decay * decay)

    def reflection(rates):
        beyond = jnp.where(lat_lane >= first_row + 8, rates, 0.0)
        running = beyond
        for k in range(6):
            step = 1 << k
            running = running + jnp.where(lat_lane >= step, pltpu.roll(running, step, 1), 0.0)
        decay = jnp.exp(-rates)
        weight = jnp.sqrt(1.0 - decay * decay)
        terms = weight * jnp.exp(-(2.0 * running - rates))
        inside = (lat_lane >= first_row + 8) & (lat_lane < 64)
        return jnp.sum(jnp.where(inside, terms, 0.0), axis=1, keepdims=True)

    span = GROUPS // CHUNKS

    def rows_of(g):
        return pl.ds(pl.multiple_of(g * 8, 8), 8)

    def chunk_rows(c):
        return pl.ds(c * span * 8, span * 8)

    def exchange(src, dst, c, sems):
        return pltpu.make_async_remote_copy(
            src_ref=src.at[chunk_rows(c)],
            dst_ref=dst.at[chunk_rows(c)],
            send_sem=sems.at[0, c],
            recv_sem=sems.at[1, c],
            device_id=partner,
            device_id_type=MESH,
        )

    near = [exchange(to_partner, near_recv, c, near_sems) for c in range(CHUNKS)]
    far = [exchange(in_send, in_recv, c, far_sems) for c in range(CHUNKS)]
    toward = jnp.where(core == 1, 1, -1)

    def chip_copy(c, d):
        target = z + toward * d
        return pltpu.make_async_remote_copy(
            src_ref=chip_send.at[chunk_rows(c)],
            dst_ref=chip_recv.at[d - 1, chunk_rows(c)],
            send_sem=chip_send_sems.at[c, d - 1],
            recv_sem=chip_recv_sems.at[c, d - 1],
            device_id=(target * 2 + core, lon),
            device_id_type=MESH,
        )

    def target_there(d):
        target = z + toward * d
        return (target >= 0) & (target < 4)

    def sender_there(d):
        sender = z - toward * d
        return (sender >= 0) & (sender < 4)

    for c in range(CHUNKS):

        @pl.loop(c * span, (c + 1) * span)
        def _(g):
            rows = rows_of(g)
            inv = lon_rate(rows)
            east_power = jnp.exp(-inv * lane_f)
            west_power = jnp.exp(-inv * jnp.maximum(97.0 - lane_f, 0.0))
            part = pl.ds(pl.multiple_of((g // 8) * 8, 8), 8)
            arriving = pltpu.roll(lon_acc[part, :], lax.rem(LANES - (g % 8) * 16, LANES), 1)
            rates = lat_rates(rows)
            decay, weight = own_factors(rates)
            north = jnp.zeros((8, LANES), jnp.float32)
            values = []
            for j in range(8):
                at = pl.ds(pl.multiple_of(g * 64 + j * 8, 8), 8)
                value = (
                    field[at, :]
                    + spread(arriving[:, j : j + 1]) * east_power
                    + spread(arriving[:, 8 + j : 9 + j]) * west_power
                )
                field[at, :] = value
                north = spread(decay[:, j : j + 1]) * north + spread(weight[:, j : j + 1]) * value
                values.append(north)
            south = jnp.zeros((8, LANES), jnp.float32)
            for j in reversed(range(8)):
                south = (
                    spread(decay[:, j : j + 1]) * south + spread(weight[:, j : j + 1]) * values[j]
                )
            through = total_between(rates, first_row, first_row + 8)
            southbound = south + spread(through * reflection(rates)) * north
            north_end[rows, :] = north
            to_partner[rows, :] = jnp.where(core == 0, north, southbound)
            own_out[rows, :] = jnp.where(core == 0, southbound, north)

        near[c].start()

    for c in range(CHUNKS):
        near[c].wait_recv()

        @pl.loop(c * span, (c + 1) * span)
        def _(g):
            rows = rows_of(g)
            through = total_between(lat_rates(rows), first_row, first_row + 8)
            chip_send[rows, :] = own_out[rows, :] + spread(through) * near_recv[rows, :]

        for d in range(1, 4):

            @pl.when(target_there(d))
            def _():
                chip_copy(c, d).start()

    for c in range(CHUNKS):
        for d in range(1, 4):

            @pl.when(sender_there(d))
            def _():
                chip_copy(c, d).wait_recv()

        @pl.loop(c * span, (c + 1) * span)
        def _(g):
            rows = rows_of(g)
            rates = lat_rates(rows)
            total = jnp.zeros((8, LANES), jnp.float32)
            for d in range(1, 4):
                low = jnp.where(core == 1, z - d + 1, z + 1) * 16
                high = jnp.where(core == 1, z, z + d) * 16
                factor = spread(total_between(rates, low, high))
                total = total + jnp.where(
                    sender_there(d), factor * chip_recv[d - 1, rows, :], 0.0
                )
            in_send[rows, :] = total

        far[c].start()

    for c in range(CHUNKS):
        far[c].wait_recv()

        @pl.loop(c * span, (c + 1) * span)
        def _(g):
            rows = rows_of(g)
            rates = lat_rates(rows)
            decay, weight = own_factors(rates)
            past = total_between(rates, partner_first, partner_first + 8)
            nearer = near_recv[rows, :] + spread(past) * in_send[rows, :]
            farther = in_recv[rows, :]
            north_in = jnp.where(core == 1, nearer, farther)
            south_sum = jnp.where(core == 1, farther, nearer)
            through = total_between(rates, first_row, first_row + 8)
            north_out = north_end[rows, :] + spread(through) * north_in
            south_in = south_sum + spread(reflection(rates)) * north_out
            north = north_in
            values = []
            for j in range(8):
                at = pl.ds(pl.multiple_of(g * 64 + j * 8, 8), 8)
                north = (
                    spread(decay[:, j : j + 1]) * north
                    + spread(weight[:, j : j + 1]) * field[at, :]
                )
                values.append(north)
            south = south_in
            results = [None] * 8 + [south_in]
            for j in reversed(range(8)):
                south = (
                    spread(decay[:, j : j + 1]) * south + spread(weight[:, j : j + 1]) * values[j]
                )
                results[j] = south
            below = (
                spread(decay[:, LANES - 1 : LANES]) * results[0]
                + spread(weight[:, LANES - 1 : LANES]) * north_in
            )
            below = jnp.where(lat == 0, 0.0, below)
            for j in range(8):
                final[pl.ds(g * 64 + j, 8, stride=8), :] = results[j]
                lower = below if j == 0 else results[j - 1]
                slopes[pl.ds(g * 64 + j, 8, stride=8), :] = (results[j + 1] - lower) * 0.5
            for j in range(8):
                whole[g * 8 + j] = final[pl.ds(pl.multiple_of(g * 64 + j * 8, 8), 8), :]

    quarter = x
    base = lax.rem(96 * quarter + 127, LANES)
    free = lane // 32 == 3 - quarter

    def pack(dest):
        def slot(i):
            return whole[source_ref[dest * SLOTS + i]]

        last = slot(3)
        for i in range(3):
            piece = pltpu.roll(slot(i), base, 1)
            extra = pltpu.roll(last, lax.rem(base + 32 * (3 - i), LANES), 1)
            blocks_out[dest, :, i * LANES : (i + 1) * LANES] = jnp.where(free, extra, piece)

    def place(o):
        oz, oc, oy, ox = o // 32, (o // 16) % 2, (o // 4) % 4, o % 4
        tlat = lax.rem(z + oz, 4) * 2 + lax.rem(core + oc, 2)
        tlon = lax.rem(y + oy, 4) * 4 + lax.rem(x + ox, 4)
        return tlat, tlon

    @pl.loop(1, 128)
    def _(i):
        tlat, tlon = place(lax.rem(i * 45, 128))
        dest = tlat * 16 + tlon
        pack(dest)
        pltpu.make_async_remote_copy(
            src_ref=blocks_out.at[dest],
            dst_ref=arrived_ref.at[me],
            send_sem=all_sems.at[0],
            recv_sem=all_sems.at[1],
            device_id=(tlat, tlon),
            device_id_type=MESH,
        ).start()

    pack(me)
    kept = pltpu.make_async_copy(blocks_out.at[me], arrived_ref.at[me], all_sems.at[2])
    kept.start()

    row = (first_row + iota((8, LANES), 0)).astype(jnp.float32) + float(NLAT_GLOBE - 64)
    latitude = math.pi * ((row + 0.5) / NLAT_GLOBE - 0.5)
    metric = 0.5 / jnp.maximum(jnp.cos(latitude), 0.2)

    @pl.loop(0, NLEV)
    def _(k):
        one = pl.ds(pl.multiple_of(k * 8, 8), 8)
        two = pl.ds(pl.multiple_of((k + NLEV) * 8, 8), 8)
        rot, div = final[one, :], final[two, :]
        rot_lon = pltpu.roll(rot, LANES - 2, 1) - rot
        div_lon = pltpu.roll(div, LANES - 2, 1) - div
        rot_lat = pltpu.roll(slopes[one, :], LANES - 1, 1)
        div_lat = pltpu.roll(slopes[two, :], LANES - 1, 1)
        padded[k] = div_lon * metric - rot_lat
        padded[k + NLEV] = rot_lon * metric + div_lat

    kept_winds = pltpu.make_async_copy(padded.at[pl.ds(0, NVL)], winds_ref, in_sem)
    kept_winds.start()

    pltpu.make_async_copy(fifteen, fifteen, lon_sems.at[0]).wait()
    for c in range(CHUNKS):
        near[c].wait_send()
        far[c].wait_send()
        for d in range(1, 4):

            @pl.when(target_there(d))
            def _():
                chip_copy(c, d).wait_send()

    kept.wait()
    kept_winds.wait()
    others = blocks_out.at[pl.ds(0, 127)]
    landed = arrived_ref.at[pl.ds(0, 127)]
    pltpu.make_async_copy(others, others, all_sems.at[0]).wait()
    pltpu.make_async_copy(landed, landed, all_sems.at[1]).wait()


def slabs_kernel(arrived_ref, winds_in_ref, slabs_ref, winds_ref):
    lane = iota((8, LANES), 1)
    block = lane // 32
    for g in range(4):
        got = [
            [arrived_ref[4 * g + l, :, c * LANES : (c + 1) * LANES] for c in range(3)]
            for l in range(4)
        ]

        def put(slot, v, value):
            at = (g * 3 + v) * LANES
            slabs_ref[slot, :, at : at + LANES] = value

        moved = []
        for c in range(3):
            for v, width in enumerate((96, 64, 32)):
                put(c, v, jnp.where(lane < width, got[v][c], got[v + 1][c]))
            merged = jnp.where(
                block == 3,
                got[0][c],
                jnp.where(block == 2, got[1][c], jnp.where(block == 1, got[2][c], got[3][c])),
            )
            moved.append(pltpu.roll(merged, 32 * (c + 1), 1))
        for v in range(3):
            parts = [moved[(4 * v + b) % 3] for b in range(4)]
            value = jnp.where(
                block == 0,
                parts[0],
                jnp.where(block == 1, parts[1], jnp.where(block == 2, parts[2], parts[3])),
            )
            put(3, v, value)
    winds_ref[...] = winds_in_ref[:, :, 0:COLS]


def shards(control, vert_band, lat_length, lon_length, band_index, owner_device):
    source = slot_sources(owner_device, 128, SLOTS)
    lengths = jnp.concatenate([lat_length, lon_length[:, None]], axis=1)
    table = jnp.pad(lengths, ((0, 10), (0, LANES - 9)), constant_values=1.0)
    band = jnp.pad(band_index.astype(jnp.float32), (0, 64))
    table = jnp.where(jnp.arange(264)[:, None] == 256, band[None, :], table)
    vmem = pltpu.VMEM
    f32 = jnp.float32
    level = (256, LANES)
    arrived, winds_wide = pl.pallas_call(
        columns_kernel,
        out_shape=(
            jax.ShapeDtypeStruct((128, 8, 3 * LANES), f32),
            jax.ShapeDtypeStruct((NVL, 8, LANES), f32),
        ),
        in_specs=[
            pl.BlockSpec(memory_space=pltpu.SMEM),
            pl.BlockSpec(memory_space=pltpu.SMEM),
            pl.BlockSpec(memory_space=vmem),
            pl.BlockSpec(memory_space=pl.ANY),
        ],
        out_specs=(pl.BlockSpec(memory_space=pl.ANY), pl.BlockSpec(memory_space=pl.ANY)),
        scratch_shapes=[
            vmem((NVL, 8, COLS), f32),
            vmem((2 * 135, 8, LANES), f32),
            vmem((2048, LANES), f32),
            vmem((2048, LANES), f32),
            vmem((2048, LANES), f32),
            vmem((256, 8, LANES), f32),
            vmem((2048, LANES), f32),
            vmem(level, f32),
            vmem((32, LANES), f32),
            vmem((16, 32, LANES), f32),
            vmem((64, LANES), f32),
            vmem(level, f32),
            vmem(level, f32),
            vmem(level, f32),
            vmem(level, f32),
            vmem((3,) + level, f32),
            vmem(level, f32),
            vmem(level, f32),
            vmem(level, f32),
            vmem((128, 8, 3 * LANES), f32),
            pltpu.SemaphoreType.DMA,
            pltpu.SemaphoreType.DMA((2,)),
            pltpu.SemaphoreType.DMA((2, CHUNKS)),
            pltpu.SemaphoreType.DMA((CHUNKS, 3)),
            pltpu.SemaphoreType.DMA((CHUNKS, 3)),
            pltpu.SemaphoreType.DMA((2, CHUNKS)),
            pltpu.SemaphoreType.DMA((3,)),
        ],
        compiler_params=pltpu.CompilerParams(collective_id=0, has_side_effects=True),
        name="columns",
    )(source, vert_band, table, control)
    slabs, winds = pl.pallas_call(
        slabs_kernel,
        grid=(8,),
        out_shape=(
            jax.ShapeDtypeStruct((SLOTS, 64, 1536), f32),
            jax.ShapeDtypeStruct((NVL, 8, COLS), f32),
        ),
        in_specs=[
            pl.BlockSpec((16, 8, 3 * LANES), lambda i: (i, 0, 0)),
            pl.BlockSpec((32, 8, LANES), lambda i: (i, 0, 0)),
        ],
        out_specs=(
            pl.BlockSpec((SLOTS, 8, 1536), lambda i: (0, i, 0)),
            pl.BlockSpec((32, 8, COLS), lambda i: (i, 0, 0)),
        ),
        name="slabs",
    )(arrived, winds_wide)
    return (winds, slabs)


def solution(mesh):
    placed = (P(None, "lat", "lon"), P(), P(), P(), P(), P())
    return jax.shard_map(
        shards,
        mesh=mesh,
        in_specs=placed,
        out_specs=(P(None, "lat", "lon"), P(("lat", "lon"), None, None)),
        check_vma=False,
    )
```

```python
import math

import jax
import jax.numpy as jnp
from jax import lax
from jax.experimental import pallas as pl
from jax.experimental.pallas import tpu as pltpu
from jax.sharding import PartitionSpec as P

NLAT_GLOBE = 768
MESH = pl.DeviceIdType.MESH
NLEV = 127
LANES = 128
WIDE = 256
COLS = 96
SLOTS = 4
STEPS = 12
HIGH = 104
CHUNKS = ((0, 6), (6, 13))
BATCHES = 2
SPREAD = 45
BF = jnp.bfloat16
F32 = jnp.float32


def iota(shape, dim):
    return lax.broadcasted_iota(jnp.int32, shape, dim)


def wide(row):
    return jnp.broadcast_to(row, (8, WIDE))


def tile(index):
    return pl.ds(pl.multiple_of(index * 8, 8), 8)


def strided(ref, start, stride, half):
    return jnp.concatenate(
        [ref[pl.ds(start + t * half, 8, stride=stride), :] for t in range(2)], axis=1
    )


def row_of(ref, index):
    return jnp.concatenate([ref[pl.ds(index + t * 64, 1), :] for t in range(2)], axis=1)


def split(value):
    high = value.astype(BF)
    return high, (value - high.astype(F32)).astype(BF)


def columns_kernel(
    band_index_ref,
    table_ref,
    control_ref,
    arrived_ref,
    winds_ref,
    control_in,
    parts_high,
    parts_low,
    band_high,
    band_low,
    mixed,
    field,
    slopes,
    natural,
    turned_high,
    turned_low,
    picks,
    by_slot,
    blocks_out,
    lengths,
    decays,
    weights,
    own_decay,
    own_weight,
    small,
    metrics,
    powers,
    east_in,
    west_in,
    lon_send,
    lon_recv,
    lon_total,
    to_partner,
    own_out,
    near_recv,
    chip_send,
    chip_recv,
    in_send,
    in_recv,
    north_end,
    in_sem,
    lon_sems,
    near_sems,
    chip_send_sems,
    chip_recv_sems,
    far_sems,
    all_sems,
):
    lat = lax.axis_index("lat")
    lon = lax.axis_index("lon")
    z, core = lat // 2, lat % 2
    y, x = lon // 4, lon % 4
    me = lat * 16 + lon
    partner = (z * 2 + 1 - core, lon)
    first_row = lat * 8

    barrier = pltpu.get_barrier_semaphore()

    @pl.loop(1, 16)
    def _(i):
        pl.semaphore_signal(
            barrier, inc=1, device_id=(lat, lax.rem(lon + i, 16)), device_id_type=MESH
        )

    @pl.loop(1, 8)
    def _(i):
        pl.semaphore_signal(
            barrier, inc=1, device_id=(lax.rem(lat + i, 8), lon), device_id_type=MESH
        )

    load = pltpu.make_async_copy(control_ref, control_in, in_sem)
    load.start()

    row8 = iota((8, WIDE), 0)
    lane = iota((8, LANES), 1)

    column = iota((8, WIDE), 1)
    kind = column // LANES
    level = column % LANES
    place_of = kind * NLEV + level
    real = level < NLEV
    targets = []
    for o in range(9):
        inside = (level + (o - 4) >= 0) & (level + (o - 4) < NLEV) & real
        targets.append(jnp.where(inside, place_of + (o - 4), -1))
    bands = [wide(table_ref[16 + o : 17 + o, :]) for o in range(9)]
    bands[4] = bands[4] + 1.0

    @pl.loop(0, 16)
    def _(r):
        pair = []
        for h in range(2):
            row = row8 + r * 16 + h * 8
            total = jnp.zeros((8, WIDE), F32)
            for o in range(9):
                total = jnp.where(targets[o] == row, bands[o], total)
            pair.append(total)
        high, low = split(jnp.concatenate(pair, axis=0))
        at = pl.ds(pl.multiple_of(r * 16, 16), 16)
        band_high[at, :] = high
        band_low[at, :] = low

    load.wait()

    @pl.loop(0, 8)
    def _(j):
        value = control_in[j]
        high, low = split(value)
        at = pl.ds(pl.multiple_of(j * COLS, 16), COLS)
        parts_high[at, :] = jnp.zeros((COLS, WIDE), BF)
        parts_low[at, :] = jnp.zeros((COLS, WIDE), BF)
        parts_high[at, 0:254] = high
        parts_low[at, 0:254] = low

    for h in range(2):
        at = slice(h * 384, h * 384 + 384)
        product = (
            jnp.dot(parts_high[at, :], band_high[...], preferred_element_type=F32)
            + jnp.dot(parts_high[at, :], band_low[...], preferred_element_type=F32)
            + jnp.dot(parts_low[at, :], band_high[...], preferred_element_type=F32)
        )
        for t in range(2):
            put = slice(t * 768 + h * 384, t * 768 + h * 384 + 384)
            mixed[put, :] = product[:, t * LANES : t * LANES + LANES]

    inv = 1.0 / wide(table_ref[8:9, :])
    row_f = row8.astype(F32)
    decay = jnp.exp(-inv)
    for r in range(STEPS):
        powers[r * 8 : r * 8 + 8, :] = jnp.exp(-float(r + 1) * inv)
    joins = []
    for step in (1, 2, 4):
        power = jnp.exp(-float(12 * step) * inv)
        joins.append(
            (step, jnp.where(row8 >= step, power, 0.0), jnp.where(row8 < 8 - step, power, 0.0))
        )

    @pl.loop(0, 8)
    def _(j):
        values = [strided(mixed, j * COLS + r, 12, 768) for r in range(STEPS)]
        west = [None] * STEPS
        west[STEPS - 1] = values[STEPS - 1]
        for r in reversed(range(STEPS - 1)):
            west[r] = decay * west[r + 1] + values[r]
        east = values[0]
        field[tile(j * 13), :] = west[0]
        for r in range(1, STEPS):
            before = decay * east
            east = before + values[r]
            field[tile(j * 13 + r), :] = before + west[r]
        west = west[0]
        for step, up, down in joins:
            east = east + up * pltpu.roll(east, step, 0)
            west = west + down * pltpu.roll(west, 8 - step, 0)
        east_in[tile(j), :] = jnp.where(row8 >= 1, pltpu.roll(east, 1, 0), 0.0)
        west_in[tile(j), :] = jnp.where(row8 < 7, pltpu.roll(west, 7, 0), 0.0)
        lon_send[pl.ds(j, 1), :] = east[7:8, :]
        lon_send[pl.ds(8 + j, 1), :] = west[0:1, :]

    pl.semaphore_wait(barrier, 22)

    @pl.loop(1, 16)
    def _(i):
        pltpu.make_async_remote_copy(
            src_ref=lon_send,
            dst_ref=lon_recv.at[lon],
            send_sem=lon_sems.at[0],
            recv_sem=lon_sems.at[1],
            device_id=(lat, lax.rem(lon + i, 16)),
            device_id_type=MESH,
        ).start()

    for b in range(8):
        lengths[b] = table_ref[b : b + 1, :]

    for j in range(64):
        value = lengths[band_index_ref[j]]
        decays[j : j + 1, :] = value[:, :LANES]
        decays[64 + j : 65 + j, :] = value[:, LANES:]

    @pl.loop(0, 16)
    def _(r):
        value = jnp.exp(-1.0 / decays[tile(r), :])
        decays[tile(r), :] = value
        weights[tile(r), :] = jnp.sqrt(1.0 - value * value)

    for j in range(8):
        own_decay[j * 8 : j * 8 + 8, :] = wide(row_of(decays, first_row + j))
        own_weight[j * 8 : j * 8 + 8, :] = wide(row_of(weights, first_row + j))

    through = jnp.ones((8, WIDE), F32)
    answer = jnp.zeros((8, WIDE), F32)
    for j in reversed(range(8)):
        value = strided(decays, j, 8, 64)
        through = through * value
        answer = value * (strided(weights, j, 8, 64) + value * answer)
    small[0:8, :] = through
    squares = through * through
    for step in (1, 2, 4):
        there = row8 < 8 - step
        answer = answer + squares * jnp.where(there, pltpu.roll(answer, 8 - step, 0), 0.0)
        squares = squares * jnp.where(there, pltpu.roll(squares, 8 - step, 0), 0.0)
    small[8:16, :] = answer
    small[16:24, :] = jnp.zeros((8, WIDE), F32)

    def block_row(index):
        return small[pl.ds(index, 1), :]

    def chip_through(chip):
        first = jnp.clip(chip, 0, 3) * 2
        return block_row(first) * block_row(first + 1)

    own_through = wide(block_row(lat))
    partner_through = wide(block_row(z * 2 + 1 - core))
    reflection = wide(block_row(8 + lat + 1))
    outward = jnp.where(core == 1, -1, 1)
    second = chip_through(z + outward)
    third = second * chip_through(z + 2 * outward)
    chip_factors = [None, wide(second), wide(third)]

    owner = wide(table_ref[9:10, :])
    real_f = jnp.where(real, 1.0, 0.0)
    earlier = jnp.where(iota((WIDE, WIDE), 0) < iota((WIDE, WIDE), 1), 1.0, 0.0).astype(BF)
    device = iota((LANES, WIDE), 0).astype(F32)
    owned = jnp.where(
        (device == jnp.broadcast_to(table_ref[9:10, :], (LANES, WIDE)))
        & (jnp.broadcast_to(real_f[0:1, :], (LANES, WIDE)) > 0.5),
        1.0,
        0.0,
    )
    before = jnp.dot(owned.astype(BF), earlier, preferred_element_type=F32)
    rank = jnp.sum(owned * before, axis=0, keepdims=True)
    slot_of = jnp.where(real, owner * float(SLOTS) + wide(rank), -1.0).astype(jnp.int32)

    def place(o):
        oz, oc, oy, ox = o // 32, (o // 16) % 2, (o // 4) % 4, o % 4
        tlat = ((z + oz) & 3) * 2 + ((core + oc) & 1)
        tlon = ((y + oy) & 3) * 4 + ((x + ox) & 3)
        return tlat, tlon

    @pl.loop(0, 32)
    def _(r):
        row = iota((16, WIDE), 0) + r * 16
        o = ((row // SLOTS) * SPREAD) & 127
        oz, oc, oy, ox = o // 32, (o // 16) & 1, (o // 4) & 3, o & 3
        tlat = ((z + oz) & 3) * 2 + ((core + oc) & 1)
        tlon = ((y + oy) & 3) * 4 + ((x + ox) & 3)
        wanted = (tlat * 16 + tlon) * SLOTS + (row & 3)
        both = jnp.concatenate([slot_of, slot_of], axis=0)
        picks[pl.ds(pl.multiple_of(r * 16, 16), 16), :] = jnp.where(both == wanted, 1.0, 0.0).astype(BF)

    fifteen = lon_recv.at[pl.ds(0, 15)]
    pltpu.make_async_copy(fifteen, fifteen, lon_sems.at[1]).wait()

    block_power = [jnp.exp(-float(96 * n) * inv) for n in range(16)]
    closing = 1.0 / (1.0 - jnp.exp(-1536.0 * inv))
    east_total = lon_send[0:8, :] * block_power[15]
    west_total = lon_send[8:16, :] * block_power[15]
    for dq in range(1, 16):
        sender = lax.rem(lon + 16 - dq, 16)
        east_total = east_total + lon_recv[sender, 0:8, :] * block_power[dq - 1]
        west_total = west_total + lon_recv[sender, 8:16, :] * block_power[15 - dq]
    east_total = east_total * closing
    west_total = west_total * closing
    lon_total[0:8, :] = east_total
    lon_total[8:16, :] = west_total
    far_power = jnp.exp(-97.0 * inv)
    lon_total[16:24, :] = east_total + decay * lon_send[8:16, :] + far_power * west_total
    lon_total[24:32, :] = west_total + decay * lon_send[0:8, :] + far_power * east_total
    segment = jnp.exp(-12.0 * row_f * inv)
    segment_back = jnp.exp(-12.0 * (7.0 - row_f) * inv)
    for j in range(8):
        at = slice(j * 8, j * 8 + 8)
        east_in[at, :] = east_in[at, :] + wide(lon_total[j : j + 1, :]) * segment
        west_in[at, :] = west_in[at, :] + wide(lon_total[8 + j : 9 + j, :]) * segment_back
        beside = jnp.where(
            row8 == 0,
            wide(lon_total[16 + j : 17 + j, :]),
            jnp.where(row8 == 1, wide(lon_total[24 + j : 25 + j, :]), 0.0),
        )
        field[(j * 13 + 12) * 8 : (j * 13 + 13) * 8, :] = beside

    def chunk_rows(c):
        low, high = CHUNKS[c]
        return pl.ds(low * 8, (high - low) * 8)

    def exchange(src, dst, c, sems):
        return pltpu.make_async_remote_copy(
            src_ref=src.at[chunk_rows(c)],
            dst_ref=dst.at[chunk_rows(c)],
            send_sem=sems.at[0, c],
            recv_sem=sems.at[1, c],
            device_id=partner,
            device_id_type=MESH,
        )

    count = len(CHUNKS)
    near = [exchange(to_partner, near_recv, c, near_sems) for c in range(count)]
    far = [exchange(in_send, in_recv, c, far_sems) for c in range(count)]
    toward = jnp.where(core == 1, 1, -1)

    def chip_copy(c, d):
        target = z + toward * d
        return pltpu.make_async_remote_copy(
            src_ref=chip_send.at[chunk_rows(c)],
            dst_ref=chip_recv.at[d - 1, chunk_rows(c)],
            send_sem=chip_send_sems.at[c, d - 1],
            recv_sem=chip_recv_sems.at[c, d - 1],
            device_id=(target * 2 + core, lon),
            device_id_type=MESH,
        )

    def target_there(d):
        target = z + toward * d
        return (target >= 0) & (target < 4)

    def sender_there(d):
        sender = z - toward * d
        return (sender >= 0) & (sender < 4)

    def own(ref, j):
        return ref[j * 8 : j * 8 + 8, :]

    def edges(g, beside):
        north = jnp.zeros((8, WIDE), F32)
        values = []
        for j in range(8):
            value = field[tile(j * 13 + g), :]
            if not beside:
                value = (
                    value
                    + own(east_in, j) * powers[tile(g), :]
                    + own(west_in, j) * powers[tile(11 - g), :]
                )
                field[tile(j * 13 + g), :] = value
            north = own(own_decay, j) * north + own(own_weight, j) * value
            values.append(north)
        south = jnp.zeros((8, WIDE), F32)
        for j in reversed(range(8)):
            south = own(own_decay, j) * south + own(own_weight, j) * values[j]
        southbound = south + own_through * reflection * north
        north_end[tile(g), :] = north
        to_partner[tile(g), :] = jnp.where(core == 0, north, southbound)
        own_out[tile(g), :] = jnp.where(core == 0, southbound, north)

    for c in range(count):
        low, high = CHUNKS[c]

        @pl.loop(low, min(high, STEPS), unroll=2)
        def _(g):
            edges(g, False)

        if high > STEPS:
            edges(STEPS, True)
        near[c].start()

    for c in range(count):
        near[c].wait_recv()
        at = slice(CHUNKS[c][0] * 8, CHUNKS[c][1] * 8)
        for g in range(*CHUNKS[c]):
            at = slice(g * 8, g * 8 + 8)
            chip_send[at, :] = own_out[at, :] + own_through * near_recv[at, :]
        for d in range(1, 4):

            @pl.when(target_there(d))
            def _():
                chip_copy(c, d).start()

    for c in range(count):
        for d in range(1, 4):

            @pl.when(sender_there(d))
            def _():
                chip_copy(c, d).wait_recv()

        for g in range(*CHUNKS[c]):
            at = slice(g * 8, g * 8 + 8)
            total = jnp.where(sender_there(1), chip_recv[0, at, :], 0.0)
            for d in (2, 3):
                total = total + jnp.where(
                    sender_there(d), chip_factors[d - 1] * chip_recv[d - 1, at, :], 0.0
                )
            in_send[at, :] = total

        far[c].start()

    below_decay = wide(row_of(decays, jnp.maximum(first_row - 1, 0)))
    below_weight = wide(row_of(weights, jnp.maximum(first_row - 1, 0)))

    def finish(g, beside):
        at = tile(g)
        nearer = near_recv[at, :] + partner_through * in_send[at, :]
        farther = in_recv[at, :]
        north_in = jnp.where(core == 1, nearer, farther)
        south_sum = jnp.where(core == 1, farther, nearer)
        north_out = north_end[at, :] + own_through * north_in
        south_in = south_sum + reflection * north_out
        north = north_in
        values = []
        for j in range(8):
            north = own(own_decay, j) * north + own(own_weight, j) * field[tile(j * 13 + g), :]
            values.append(north)
        south = south_in
        results = [None] * 8 + [south_in]
        for j in reversed(range(8)):
            south = own(own_decay, j) * south + own(own_weight, j) * values[j]
            results[j] = south
        below = below_decay * results[0] + below_weight * north_in
        below = jnp.where(lat == 0, 0.0, below)
        for j in range(8):
            field[tile(j * 13 + g), :] = results[j]
            if not beside:
                lower = below if j == 0 else results[j - 1]
                slopes[tile(j * 12 + g), :] = (results[j + 1] - lower) * 0.5
                for t in range(2):
                    natural[pl.ds(t * 768 + j * COLS + g, 8, stride=12), :] = results[j][
                        :, t * LANES : t * LANES + LANES
                    ]

    for c in range(count):
        low, high = CHUNKS[c]
        far[c].wait_recv()

        @pl.loop(low, min(high, STEPS), unroll=2)
        def _(g):
            finish(g, False)

        if high > STEPS:
            finish(STEPS, True)

    quarter = x
    free = lane // 32 == 3 - quarter

    @pl.loop(0, 8)
    def _(j):
        for m in range(3):
            start = pl.multiple_of(j * COLS + m * 32, 32)
            high, low = split(
                jnp.concatenate([natural[pl.ds(start + t * 768, 32), :] for t in range(2)], axis=1)
            )
            at = pl.ds(pl.multiple_of(j * LANES + ((3 * quarter + m) & 3) * 32, 32), 32)
            turned_high[at, :] = high
            turned_low[at, :] = low
        at = pl.ds(pl.multiple_of(j * LANES + (3 - quarter) * 32, 32), 32)
        turned_high[at, :] = jnp.zeros((32, WIDE), BF)
        turned_low[at, :] = jnp.zeros((32, WIDE), BF)

    across = (((1,), (1,)), ((), ()))
    per_batch = 128 // BATCHES
    rows_batch = per_batch * SLOTS
    for b in range(BATCHES):
        chosen = picks[b * rows_batch : (b + 1) * rows_batch, :]
        for jp in range(4):
            at = slice(jp * WIDE, jp * WIDE + WIDE)
            out = lax.dot_general(
                chosen, turned_high[at, :], across, preferred_element_type=F32
            ) + lax.dot_general(chosen, turned_low[at, :], across, preferred_element_type=F32)
            for h in range(2):
                for q in range(rows_batch // 8):
                    by_slot[
                        pl.ds((b * rows_batch + q * 8) * 8 + jp * 2 + h, 8, stride=8), :
                    ] = out[q * 8 : q * 8 + 8, h * LANES : h * LANES + LANES]

        @pl.loop(b * per_batch, (b + 1) * per_batch, unroll=2)
        def _(u):
            last = by_slot[tile(u * SLOTS + 3), :]
            for i in range(3):
                extra = pltpu.roll(last, 32 * (3 - i), 1)
                blocks_out[u, :, i * LANES : (i + 1) * LANES] = jnp.where(
                    free, extra, by_slot[tile(u * SLOTS + i), :]
                )

        @pl.loop(max(b * per_batch, 1), (b + 1) * per_batch)
        def _(u):
            tlat, tlon = place((u * SPREAD) & 127)
            pltpu.make_async_remote_copy(
                src_ref=blocks_out.at[u],
                dst_ref=arrived_ref.at[me],
                send_sem=all_sems.at[0],
                recv_sem=all_sems.at[1],
                device_id=(tlat, tlon),
                device_id_type=MESH,
            ).start()

    kept = pltpu.make_async_copy(blocks_out.at[0], arrived_ref.at[me], all_sems.at[2])
    kept.start()

    latitude_row = (first_row + row8).astype(F32) + float(NLAT_GLOBE - 64)
    latitude = math.pi * ((latitude_row + 0.5) / NLAT_GLOBE - 0.5)
    metrics[...] = (0.5 / jnp.maximum(jnp.cos(latitude), 0.2))[:, :LANES]

    @pl.loop(0, 8)
    def _(j):
        metric = jnp.broadcast_to(metrics[pl.ds(j, 1), :], (8, LANES))
        beside = field[tile(j * 13 + 12), :]
        for g in range(STEPS):
            if g == STEPS - 1:
                after = jnp.where(
                    row8 == 7, wide(beside[1:2, :]), pltpu.roll(field[tile(j * 13), :], 7, 0)
                )
            else:
                after = field[tile(j * 13 + g + 1), :]
            if g == 0:
                ahead = jnp.where(
                    row8 == 0, wide(beside[0:1, :]), pltpu.roll(field[tile(j * 13 + 11), :], 1, 0)
                )
            else:
                ahead = field[tile(j * 13 + g - 1), :]
            along = after - ahead
            slope = slopes[tile(j * 12 + g), :]
            eastern = along[:, LANES:] * metric - slope[:, :LANES]
            northern = pltpu.roll(along[:, :LANES] * metric + slope[:, LANES:], LANES - 1, 1)
            at = j * COLS + g
            mixed[pl.ds(at, 8, stride=12), :] = jnp.where(lane < NLEV, eastern, northern)
            mixed[pl.ds(768 + at, 8, stride=12), :] = northern

    kept_winds = pltpu.make_async_copy(mixed, winds_ref, in_sem)
    kept_winds.start()

    pltpu.make_async_copy(fifteen, fifteen, lon_sems.at[0]).wait()
    for c in range(count):
        near[c].wait_send()
        far[c].wait_send()
        for d in range(1, 4):

            @pl.when(target_there(d))
            def _():
                chip_copy(c, d).wait_send()

    kept.wait()
    kept_winds.wait()
    others = blocks_out.at[pl.ds(0, 127)]
    landed = arrived_ref.at[pl.ds(0, 127)]
    pltpu.make_async_copy(others, others, all_sems.at[0]).wait()
    pltpu.make_async_copy(landed, landed, all_sems.at[1]).wait()


def slabs_kernel(arrived_ref, low_ref, high_ref, slabs_ref, winds_ref):
    lane = iota((8, LANES), 1)
    block = lane // 32
    for g in range(4):
        got = [
            [arrived_ref[4 * g + l, :, c * LANES : (c + 1) * LANES] for c in range(3)]
            for l in range(4)
        ]

        def put(slot, v, value):
            at = (g * 3 + v) * LANES
            slabs_ref[slot, :, at : at + LANES] = value

        moved = []
        for c in range(3):
            for v, width in enumerate((96, 64, 32)):
                put(c, v, jnp.where(lane < width, got[v][c], got[v + 1][c]))
            merged = jnp.where(
                block == 3,
                got[0][c],
                jnp.where(block == 2, got[1][c], jnp.where(block == 1, got[2][c], got[3][c])),
            )
            moved.append(pltpu.roll(merged, 32 * (c + 1), 1))
        for v in range(3):
            parts = [moved[(4 * v + b) % 3] for b in range(4)]
            value = jnp.where(
                block == 0,
                parts[0],
                jnp.where(block == 1, parts[1], jnp.where(block == 2, parts[2], parts[3])),
            )
            put(3, v, value)
    winds_ref[0, :, 0:LANES] = low_ref[...]
    winds_ref[0, :, LANES : 2 * NLEV] = high_ref[:, 0 : 2 * NLEV - LANES]


def padded_rows(rows, fill):
    pairs = rows.reshape(rows.shape[0], 2, NLEV)
    return jnp.pad(pairs, ((0, 0), (0, 0), (0, 1)), constant_values=fill).reshape(-1, WIDE)


def shards(control, vert_band, lat_length, lon_length, band_index, owner_device):
    rows = jnp.concatenate(
        [lat_length.T, lon_length[None, :], owner_device.T.astype(F32)], axis=0
    )
    table = jnp.concatenate(
        [
            jnp.pad(padded_rows(rows, 1.0), ((0, 6), (0, 0))),
            jnp.pad(
                jnp.pad(vert_band.transpose(1, 0, 2), ((0, 0), (0, 0), (0, 1))).reshape(9, WIDE),
                ((0, 7), (0, 0)),
            ),
        ],
        axis=0,
    )
    vmem = pltpu.VMEM
    edge = vmem((HIGH, WIDE), F32)
    dma = pltpu.SemaphoreType.DMA
    count = len(CHUNKS)
    arrived, winds_wide = pl.pallas_call(
        columns_kernel,
        out_shape=(
            jax.ShapeDtypeStruct((128, 8, 3 * LANES), F32),
            jax.ShapeDtypeStruct((16 * COLS, LANES), F32),
        ),
        in_specs=[
            pl.BlockSpec(memory_space=pltpu.SMEM),
            pl.BlockSpec(memory_space=vmem),
            pl.BlockSpec(memory_space=pl.ANY),
        ],
        out_specs=(pl.BlockSpec(memory_space=pl.ANY), pl.BlockSpec(memory_space=pl.ANY)),
        scratch_shapes=[
            vmem((8, COLS, 2 * NLEV), F32),
            vmem((8 * COLS, WIDE), BF),
            vmem((8 * COLS, WIDE), BF),
            vmem((WIDE, WIDE), BF),
            vmem((WIDE, WIDE), BF),
            vmem((16 * COLS, LANES), F32),
            vmem((8 * HIGH, WIDE), F32),
            vmem((8 * COLS, WIDE), F32),
            vmem((16 * COLS, LANES), F32),
            vmem((8 * LANES, WIDE), BF),
            vmem((8 * LANES, WIDE), BF),
            vmem((512, WIDE), BF),
            vmem((4096, LANES), F32),
            vmem((128, 8, 3 * LANES), F32),
            vmem((8, 1, WIDE), F32),
            vmem((128, LANES), F32),
            vmem((128, LANES), F32),
            vmem((64, WIDE), F32),
            vmem((64, WIDE), F32),
            vmem((32, WIDE), F32),
            vmem((8, LANES), F32),
            vmem((COLS, WIDE), F32),
            vmem((64, WIDE), F32),
            vmem((64, WIDE), F32),
            vmem((16, WIDE), F32),
            vmem((16, 16, WIDE), F32),
            vmem((32, WIDE), F32),
            edge,
            edge,
            edge,
            edge,
            vmem((3, HIGH, WIDE), F32),
            edge,
            edge,
            edge,
            dma,
            dma((2,)),
            dma((2, count)),
            dma((count, 3)),
            dma((count, 3)),
            dma((2, count)),
            dma((3,)),
        ],
        compiler_params=pltpu.CompilerParams(collective_id=0, has_side_effects=True),
        name="columns",
    )(band_index, table, control.transpose(1, 2, 0))
    slabs, winds = pl.pallas_call(
        slabs_kernel,
        grid=(8,),
        out_shape=(
            jax.ShapeDtypeStruct((SLOTS, 64, 1536), F32),
            jax.ShapeDtypeStruct((8, COLS, 2 * NLEV), F32),
        ),
        in_specs=[
            pl.BlockSpec((16, 8, 3 * LANES), lambda i: (i, 0, 0)),
            pl.BlockSpec((COLS, LANES), lambda i: (i, 0)),
            pl.BlockSpec((COLS, LANES), lambda i: (8 + i, 0)),
        ],
        out_specs=(
            pl.BlockSpec((SLOTS, 8, 1536), lambda i: (0, i, 0)),
            pl.BlockSpec((1, COLS, 2 * NLEV), lambda i: (i, 0, 0)),
        ),
        name="slabs",
    )(arrived, winds_wide, winds_wide)
    return (winds.transpose(2, 0, 1), slabs)


def solution(mesh):
    placed = (P(None, "lat", "lon"), P(), P(), P(), P(), P())
    return jax.shard_map(
        shards,
        mesh=mesh,
        in_specs=placed,
        out_specs=(P(None, "lat", "lon"), P(("lat", "lon"), None, None)),
        check_vma=False,
    )
```

```python
import math

import jax
import jax.numpy as jnp
from jax import lax
from jax.experimental import pallas as pl
from jax.experimental.pallas import tpu as pltpu
from jax.sharding import PartitionSpec as P

NLAT_GLOBE = 768
MESH = pl.DeviceIdType.MESH
NLEV = 127
LANES = 128
WIDE = 256
COLS = 96
SLOTS = 4
STEPS = 12
HIGH = 104
CHUNKS = ((0, 6), (6, 13))
BATCHES = 2
SPREAD = 45
LATS = 4
BF = jnp.bfloat16
F32 = jnp.float32


def iota(shape, dim):
    return lax.broadcasted_iota(jnp.int32, shape, dim)


def wide(row):
    return jnp.broadcast_to(row, (8, WIDE))


def tile(index):
    return pl.ds(pl.multiple_of(index * 8, 8), 8)


def strided(ref, start, stride, half):
    return jnp.concatenate(
        [ref[pl.ds(start + t * half, 8, stride=stride), :] for t in range(2)], axis=1
    )


def row_of(ref, index):
    return jnp.concatenate([ref[pl.ds(index + t * 64, 1), :] for t in range(2)], axis=1)


def split(value):
    high = value.astype(BF)
    return high, (value - high.astype(F32)).astype(BF)


def columns_kernel(
    band_index_ref,
    lat_ref,
    lon_ref,
    band_ref,
    owner_ref,
    control_ref,
    arrived_ref,
    winds_ref,
    control_in,
    lat_in,
    lon_in,
    band_in,
    owner_in,
    table_ref,
    parts_high,
    parts_low,
    band_high,
    band_low,
    mixed,
    field,
    slopes,
    natural,
    turned_high,
    turned_low,
    picks,
    by_slot,
    blocks_out,
    lengths,
    decays,
    weights,
    own_decay,
    own_weight,
    small,
    metrics,
    powers,
    east_in,
    west_in,
    lon_send,
    lon_recv,
    lon_total,
    sides,
    side_send,
    side_recv,
    east_all,
    west_all,
    beside_all,
    to_partner,
    own_out,
    near_recv,
    chip_send,
    chip_recv,
    in_send,
    in_recv,
    north_end,
    in_sem,
    raw_sems,
    lon_sems,
    side_sems,
    near_sems,
    chip_send_sems,
    chip_recv_sems,
    far_sems,
    all_sems,
):
    lat = lax.axis_index("lat")
    lon = lax.axis_index("lon")
    z, core = lat // 2, lat % 2
    y, x = lon // 4, lon % 4
    me = lat * 16 + lon
    partner = (z * 2 + 1 - core, lon)
    first_row = lat * 8

    barrier = pltpu.get_barrier_semaphore()

    @pl.loop(1, 16)
    def _(i):
        pl.semaphore_signal(
            barrier, inc=1, device_id=(lat, lax.rem(lon + i, 16)), device_id_type=MESH
        )

    @pl.loop(1, 8)
    def _(i):
        pl.semaphore_signal(
            barrier, inc=1, device_id=(lax.rem(lat + i, 8), lon), device_id_type=MESH
        )

    load = pltpu.make_async_copy(control_ref, control_in, in_sem)
    load.start()
    raw = [
        pltpu.make_async_copy(src, dst, raw_sems.at[i])
        for i, (src, dst) in enumerate(
            ((lat_ref, lat_in), (lon_ref, lon_in), (band_ref, band_in), (owner_ref, owner_in))
        )
    ]
    for copy in raw:
        copy.start()

    row8 = iota((8, WIDE), 0)
    lane = iota((8, LANES), 1)

    for copy in raw:
        copy.wait()
    table_ref[...] = jnp.ones((32, WIDE), F32)
    table_ref[0:8, 0 : 2 * NLEV] = lat_in[...]
    table_ref[8:9, 0 : 2 * NLEV] = lon_in[...]
    table_ref[9:10, 0 : 2 * NLEV] = owner_in[...].astype(F32)
    for h in range(2):
        at = slice(h * 8, h * 8 + 8)
        first, second = table_ref[at, 0:LANES], table_ref[at, LANES:WIDE]
        moved = jnp.where(lane == 0, pltpu.roll(first, 1, 1), pltpu.roll(second, 1, 1))
        table_ref[at, 0:LANES] = jnp.where(lane < NLEV, first, 1.0)
        table_ref[at, LANES:WIDE] = jnp.where(lane < NLEV, moved, 1.0)
    for o in range(9):
        table_ref[16 + o : 17 + o, 0:NLEV] = band_in[o, 0:1, :]
        table_ref[16 + o : 17 + o, LANES : LANES + NLEV] = band_in[o, 1:2, :]

    column = iota((8, WIDE), 1)
    kind = column // LANES
    level = column % LANES
    place_of = kind * NLEV + level
    real = level < NLEV
    targets = []
    for o in range(9):
        inside = (level + (o - 4) >= 0) & (level + (o - 4) < NLEV) & real
        targets.append(jnp.where(inside, place_of + (o - 4), -1))
    bands = [wide(table_ref[16 + o : 17 + o, :]) for o in range(9)]
    bands[4] = bands[4] + 1.0

    @pl.loop(0, 16)
    def _(r):
        pair = []
        for h in range(2):
            row = row8 + r * 16 + h * 8
            total = jnp.zeros((8, WIDE), F32)
            for o in range(9):
                total = jnp.where(targets[o] == row, bands[o], total)
            pair.append(total)
        high, low = split(jnp.concatenate(pair, axis=0))
        at = pl.ds(pl.multiple_of(r * 16, 16), 16)
        band_high[at, :] = high
        band_low[at, :] = low

    load.wait()

    @pl.loop(0, 8)
    def _(j):
        value = control_in[j]
        high, low = split(value)
        at = pl.ds(pl.multiple_of(j * COLS, 16), COLS)
        parts_high[at, :] = jnp.zeros((COLS, WIDE), BF)
        parts_low[at, :] = jnp.zeros((COLS, WIDE), BF)
        parts_high[at, 0:254] = high
        parts_low[at, 0:254] = low

    for h in range(2):
        at = slice(h * 384, h * 384 + 384)
        product = (
            jnp.dot(parts_high[at, :], band_high[...], preferred_element_type=F32)
            + jnp.dot(parts_high[at, :], band_low[...], preferred_element_type=F32)
            + jnp.dot(parts_low[at, :], band_high[...], preferred_element_type=F32)
        )
        for t in range(2):
            put = slice(t * 768 + h * 384, t * 768 + h * 384 + 384)
            mixed[put, :] = product[:, t * LANES : t * LANES + LANES]

    inv = 1.0 / wide(table_ref[8:9, :])
    row_f = row8.astype(F32)
    decay = jnp.exp(-inv)
    for r in range(STEPS):
        powers[r * 8 : r * 8 + 8, :] = jnp.exp(-float(r + 1) * inv)
    joins = []
    for step in (1, 2, 4):
        power = jnp.exp(-float(12 * step) * inv)
        joins.append(
            (step, jnp.where(row8 >= step, power, 0.0), jnp.where(row8 < 8 - step, power, 0.0))
        )

    @pl.loop(0, 8)
    def _(j):
        values = [strided(mixed, j * COLS + r, 12, 768) for r in range(STEPS)]
        west = [None] * STEPS
        west[STEPS - 1] = values[STEPS - 1]
        for r in reversed(range(STEPS - 1)):
            west[r] = decay * west[r + 1] + values[r]
        east = values[0]
        field[tile(j * 13), :] = west[0]
        for r in range(1, STEPS):
            before = decay * east
            east = before + values[r]
            field[tile(j * 13 + r), :] = before + west[r]
        west = west[0]
        for step, up, down in joins:
            east = east + up * pltpu.roll(east, step, 0)
            west = west + down * pltpu.roll(west, 8 - step, 0)
        east_in[tile(j), :] = jnp.where(row8 >= 1, pltpu.roll(east, 1, 0), 0.0)
        west_in[tile(j), :] = jnp.where(row8 < 7, pltpu.roll(west, 7, 0), 0.0)
        lon_send[pl.ds(j, 1), :] = east[7:8, :]
        lon_send[pl.ds(8 + j, 1), :] = west[0:1, :]

    for b in range(8):
        lengths[b] = table_ref[b : b + 1, :]

    for j in range(64):
        value = lengths[band_index_ref[j]]
        decays[j : j + 1, :] = value[:, :LANES]
        decays[64 + j : 65 + j, :] = value[:, LANES:]

    @pl.loop(0, 16)
    def _(r):
        value = jnp.exp(-1.0 / decays[tile(r), :])
        decays[tile(r), :] = value
        weights[tile(r), :] = jnp.sqrt(1.0 - value * value)

    for j in range(8):
        own_decay[j * 8 : j * 8 + 8, :] = wide(row_of(decays, first_row + j))
        own_weight[j * 8 : j * 8 + 8, :] = wide(row_of(weights, first_row + j))

    through = jnp.ones((8, WIDE), F32)
    answer = jnp.zeros((8, WIDE), F32)
    for j in reversed(range(8)):
        value = strided(decays, j, 8, 64)
        through = through * value
        answer = value * (strided(weights, j, 8, 64) + value * answer)
    small[0:8, :] = through
    squares = through * through
    for step in (1, 2, 4):
        there = row8 < 8 - step
        answer = answer + squares * jnp.where(there, pltpu.roll(answer, 8 - step, 0), 0.0)
        squares = squares * jnp.where(there, pltpu.roll(squares, 8 - step, 0), 0.0)
    small[8:16, :] = answer
    small[16:24, :] = jnp.zeros((8, WIDE), F32)

    def block_row(index):
        return small[pl.ds(index, 1), :]

    def chip_through(chip):
        first = jnp.clip(chip, 0, 3) * 2
        return block_row(first) * block_row(first + 1)

    own_through = wide(block_row(lat))
    partner_through = wide(block_row(z * 2 + 1 - core))
    reflection = wide(block_row(8 + lat + 1))
    outward = jnp.where(core == 1, -1, 1)
    second = chip_through(z + outward)
    third = second * chip_through(z + 2 * outward)
    chip_factors = [None, wide(second), wide(third)]

    for j in range(8):
        field[(j * 13 + 12) * 8 : (j * 13 + 13) * 8, :] = decay * jnp.where(
            row8 == 0,
            wide(lon_send[8 + j : 9 + j, :]),
            jnp.where(row8 == 1, wide(lon_send[j : j + 1, :]), 0.0),
        )

    def chunk_rows(c):
        low, high = CHUNKS[c]
        return pl.ds(low * 8, (high - low) * 8)

    def exchange(src, dst, c, sems):
        return pltpu.make_async_remote_copy(
            src_ref=src.at[chunk_rows(c)],
            dst_ref=dst.at[chunk_rows(c)],
            send_sem=sems.at[0, c],
            recv_sem=sems.at[1, c],
            device_id=partner,
            device_id_type=MESH,
        )

    count = len(CHUNKS)
    near = [exchange(to_partner, near_recv, c, near_sems) for c in range(count)]
    far = [exchange(in_send, in_recv, c, far_sems) for c in range(count)]
    toward = jnp.where(core == 1, 1, -1)

    def chip_copy(c, d):
        target = z + toward * d
        return pltpu.make_async_remote_copy(
            src_ref=chip_send.at[chunk_rows(c)],
            dst_ref=chip_recv.at[d - 1, chunk_rows(c)],
            send_sem=chip_send_sems.at[c, d - 1],
            recv_sem=chip_recv_sems.at[c, d - 1],
            device_id=(target * 2 + core, lon),
            device_id_type=MESH,
        )

    def target_there(d):
        target = z + toward * d
        return (target >= 0) & (target < 4)

    def sender_there(d):
        sender = z - toward * d
        return (sender >= 0) & (sender < 4)

    def own(ref, j):
        return ref[j * 8 : j * 8 + 8, :]

    side = None

    def edges(g, beside):
        north = jnp.zeros((8, WIDE), F32)
        values = []
        for j in range(8):
            value = sides[tile(j), :] if g is side else field[tile(j * 13 + g), :]
            if not beside:
                value = (
                    value
                    + own(east_in, j) * powers[tile(g), :]
                    + own(west_in, j) * powers[tile(11 - g), :]
                )
                field[tile(j * 13 + g), :] = value
            north = own(own_decay, j) * north + own(own_weight, j) * value
            values.append(north)
        south = jnp.zeros((8, WIDE), F32)
        for j in reversed(range(8)):
            south = own(own_decay, j) * south + own(own_weight, j) * values[j]
        southbound = south + own_through * reflection * north
        if g is side:
            return north, southbound
        north_end[tile(g), :] = north
        to_partner[tile(g), :] = jnp.where(core == 0, north, southbound)
        own_out[tile(g), :] = jnp.where(core == 0, southbound, north)

    for c in range(count):
        low, high = CHUNKS[c]

        @pl.loop(low, min(high, STEPS), unroll=2)
        def _(g):
            edges(g, False)

        if high > STEPS:
            edges(STEPS, True)

    pl.semaphore_wait(barrier, 22)

    @pl.loop(1, 16)
    def _(i):
        pltpu.make_async_remote_copy(
            src_ref=lon_send,
            dst_ref=lon_recv.at[lon],
            send_sem=lon_sems.at[0],
            recv_sem=lon_sems.at[1],
            device_id=(lat, lax.rem(lon + i, 16)),
            device_id_type=MESH,
        ).start()

    for c in range(count):
        near[c].start()

    for c in range(count):
        near[c].wait_recv()
        at = slice(CHUNKS[c][0] * 8, CHUNKS[c][1] * 8)
        for g in range(*CHUNKS[c]):
            at = slice(g * 8, g * 8 + 8)
            chip_send[at, :] = own_out[at, :] + own_through * near_recv[at, :]
        for d in range(1, 4):

            @pl.when(target_there(d))
            def _():
                chip_copy(c, d).start()

    fifteen = lon_recv.at[pl.ds(0, 15)]
    pltpu.make_async_copy(fifteen, fifteen, lon_sems.at[1]).wait()

    block_power = [jnp.exp(-float(96 * n) * inv) for n in range(16)]
    closing = 1.0 / (1.0 - jnp.exp(-1536.0 * inv))
    east_total = lon_send[0:8, :] * block_power[15]
    west_total = lon_send[8:16, :] * block_power[15]
    for dq in range(1, 16):
        sender = lax.rem(lon + 16 - dq, 16)
        east_total = east_total + lon_recv[sender, 0:8, :] * block_power[dq - 1]
        west_total = west_total + lon_recv[sender, 8:16, :] * block_power[15 - dq]
    east_total = east_total * closing
    west_total = west_total * closing

    lon_total[0:8, :] = east_total
    lon_total[8:16, :] = west_total
    for j in range(8):
        sides[j * 8 : j * 8 + 8, :] = jnp.where(
            row8 == 0,
            wide(lon_total[j : j + 1, :]),
            jnp.where(row8 == 1, wide(lon_total[8 + j : 9 + j, :]), 0.0),
        )
    side_north, side_south = edges(side, True)
    side_send[...] = jnp.where(row8 < 2, side_north, pltpu.roll(side_south, 2, 0))

    @pl.loop(1, 8)
    def _(i):
        pltpu.make_async_remote_copy(
            src_ref=side_send,
            dst_ref=side_recv.at[lat],
            send_sem=side_sems.at[0],
            recv_sem=side_sems.at[1],
            device_id=(lax.rem(lat + i, 8), lon),
            device_id_type=MESH,
        ).start()

    owner = wide(table_ref[9:10, :])
    real_f = jnp.where(real, 1.0, 0.0)
    earlier = jnp.where(iota((WIDE, WIDE), 0) < iota((WIDE, WIDE), 1), 1.0, 0.0).astype(BF)
    device = iota((LANES, WIDE), 0).astype(F32)
    owned = jnp.where(
        (device == jnp.broadcast_to(table_ref[9:10, :], (LANES, WIDE)))
        & (jnp.broadcast_to(real_f[0:1, :], (LANES, WIDE)) > 0.5),
        1.0,
        0.0,
    )
    before = jnp.dot(owned.astype(BF), earlier, preferred_element_type=F32)
    rank = jnp.sum(owned * before, axis=0, keepdims=True)
    slot_of = jnp.where(real, owner * float(SLOTS) + wide(rank), -1.0).astype(jnp.int32)

    def place(o):
        oz, oc, oy, ox = o // 32, (o // 16) % 2, (o // 4) % 4, o % 4
        tlat = ((z + oz) & 3) * 2 + ((core + oc) & 1)
        tlon = ((y + oy) & 3) * 4 + ((x + ox) & 3)
        return tlat, tlon

    @pl.loop(0, 32)
    def _(r):
        row = iota((16, WIDE), 0) + r * 16
        o = ((row // SLOTS) * SPREAD) & 127
        oz, oc, oy, ox = o // 32, (o // 16) & 1, (o // 4) & 3, o & 3
        tlat = ((z + oz) & 3) * 2 + ((core + oc) & 1)
        tlon = ((y + oy) & 3) * 4 + ((x + ox) & 3)
        wanted = (tlat * 16 + tlon) * SLOTS + (row & 3)
        both = jnp.concatenate([slot_of, slot_of], axis=0)
        picks[pl.ds(pl.multiple_of(r * 16, 16), 16), :] = jnp.where(both == wanted, 1.0, 0.0).astype(BF)

    for c in range(count):
        for d in range(1, 4):

            @pl.when(sender_there(d))
            def _():
                chip_copy(c, d).wait_recv()

        for g in range(*CHUNKS[c]):
            at = slice(g * 8, g * 8 + 8)
            total = jnp.where(sender_there(1), chip_recv[0, at, :], 0.0)
            for d in (2, 3):
                total = total + jnp.where(
                    sender_there(d), chip_factors[d - 1] * chip_recv[d - 1, at, :], 0.0
                )
            in_send[at, :] = total

        far[c].start()

    below_decay = wide(row_of(decays, jnp.maximum(first_row - 1, 0)))
    below_weight = wide(row_of(weights, jnp.maximum(first_row - 1, 0)))

    seven = side_recv.at[pl.ds(0, 7)]
    pltpu.make_async_copy(seven, seven, side_sems.at[1]).wait()
    side_in = jnp.zeros((8, WIDE), F32)
    for p in range(7):
        side_in = jnp.where(p < lat, wide(small[p : p + 1, :]) * side_in + side_recv[p], side_in)
    side_back = jnp.zeros((8, WIDE), F32)
    for p in reversed(range(1, 8)):
        side_back = jnp.where(
            p > lat, wide(small[p : p + 1, :]) * side_back + side_recv[p], side_back
        )
    side_back = pltpu.roll(side_back, 6, 0) + reflection * (side_north + own_through * side_in)
    north = side_in
    values = []
    for j in range(8):
        north = own(own_decay, j) * north + own(own_weight, j) * own(sides, j)
        values.append(north)
    south = side_back
    rows = [None] * 8 + [side_back]
    for j in reversed(range(8)):
        south = own(own_decay, j) * south + own(own_weight, j) * values[j]
        rows[j] = south
    edge_row = below_decay * rows[0] + below_weight * side_in
    rows = [jnp.where(lat == 0, 0.0, edge_row)] + rows
    far_power = jnp.exp(-97.0 * inv)
    segment = jnp.exp(-12.0 * row_f * inv)
    segment_back = jnp.exp(-12.0 * (7.0 - row_f) * inv)
    east_beside = jnp.where(row8 == 0, 1.0, far_power)
    west_beside = jnp.where(row8 == 0, far_power, 1.0)
    for j in range(10):
        at = slice(j * 8, j * 8 + 8)
        from_west, from_east = wide(rows[j][0:1, :]), wide(rows[j][1:2, :])
        east_all[at, :] = from_west * segment
        west_all[at, :] = from_east * segment_back
        if 1 <= j <= 8:
            beside_all[(j - 1) * 8 : j * 8, :] = (
                from_west * east_beside + from_east * west_beside
            )

    def finish(g, beside):
        at = tile(g)
        nearer = near_recv[at, :] + partner_through * in_send[at, :]
        farther = in_recv[at, :]
        north_in = jnp.where(core == 1, nearer, farther)
        south_sum = jnp.where(core == 1, farther, nearer)
        north_out = north_end[at, :] + own_through * north_in
        south_in = south_sum + reflection * north_out
        north = north_in
        values = []
        for j in range(8):
            north = own(own_decay, j) * north + own(own_weight, j) * field[tile(j * 13 + g), :]
            values.append(north)
        south = south_in
        results = [None] * 8 + [south_in]
        for j in reversed(range(8)):
            south = own(own_decay, j) * south + own(own_weight, j) * values[j]
            results[j] = south
        below = below_decay * results[0] + below_weight * north_in
        below = jnp.where(lat == 0, 0.0, below)
        if beside:
            for j in range(8):
                field[tile(j * 13 + g), :] = results[j] + own(beside_all, j)
            return
        toward_east, toward_west = powers[tile(g), :], powers[tile(11 - g), :]
        results = [
            value + own(east_all, j) * toward_east + own(west_all, j) * toward_west
            for j, value in enumerate([below] + results)
        ]
        below, results = results[0], results[1:]
        for j in range(8):
            field[tile(j * 13 + g), :] = results[j]
            if not beside:
                lower = below if j == 0 else results[j - 1]
                slopes[tile(j * 12 + g), :] = (results[j + 1] - lower) * 0.5
                for t in range(2):
                    natural[pl.ds(t * 768 + j * COLS + g, 8, stride=12), :] = results[j][
                        :, t * LANES : t * LANES + LANES
                    ]

    for c in range(count):
        low, high = CHUNKS[c]
        far[c].wait_recv()

        @pl.loop(low, min(high, STEPS), unroll=2)
        def _(g):
            finish(g, False)

        if high > STEPS:
            finish(STEPS, True)

    quarter = x
    free = lane // 32 == 3 - quarter

    @pl.loop(0, 8)
    def _(j):
        for m in range(3):
            start = pl.multiple_of(j * COLS + m * 32, 32)
            high, low = split(
                jnp.concatenate([natural[pl.ds(start + t * 768, 32), :] for t in range(2)], axis=1)
            )
            at = pl.ds(pl.multiple_of(j * LANES + ((3 * quarter + m) & 3) * 32, 32), 32)
            turned_high[at, :] = high
            turned_low[at, :] = low
        at = pl.ds(pl.multiple_of(j * LANES + (3 - quarter) * 32, 32), 32)
        turned_high[at, :] = jnp.zeros((32, WIDE), BF)
        turned_low[at, :] = jnp.zeros((32, WIDE), BF)

    across = (((1,), (1,)), ((), ()))
    per_batch = 128 // BATCHES
    rows_batch = per_batch * SLOTS
    for b in range(BATCHES):
        chosen = picks[b * rows_batch : (b + 1) * rows_batch, :]
        for jp in range(4):
            at = slice(jp * WIDE, jp * WIDE + WIDE)
            out = lax.dot_general(
                chosen, turned_high[at, :], across, preferred_element_type=F32
            ) + lax.dot_general(chosen, turned_low[at, :], across, preferred_element_type=F32)
            for h in range(2):
                for q in range(rows_batch // 8):
                    by_slot[
                        pl.ds((b * rows_batch + q * 8) * 8 + jp * 2 + h, 8, stride=8), :
                    ] = out[q * 8 : q * 8 + 8, h * LANES : h * LANES + LANES]

        @pl.loop(b * per_batch, (b + 1) * per_batch, unroll=2)
        def _(u):
            last = by_slot[tile(u * SLOTS + 3), :]
            for i in range(3):
                extra = pltpu.roll(last, 32 * (3 - i), 1)
                blocks_out[u, :, i * LANES : (i + 1) * LANES] = jnp.where(
                    free, extra, by_slot[tile(u * SLOTS + i), :]
                )

        @pl.loop(max(b * per_batch, 1), (b + 1) * per_batch)
        def _(u):
            tlat, tlon = place((u * SPREAD) & 127)
            pltpu.make_async_remote_copy(
                src_ref=blocks_out.at[u],
                dst_ref=arrived_ref.at[me],
                send_sem=all_sems.at[0],
                recv_sem=all_sems.at[1],
                device_id=(tlat, tlon),
                device_id_type=MESH,
            ).start()

    kept = pltpu.make_async_copy(blocks_out.at[0], arrived_ref.at[me], all_sems.at[2])
    kept.start()

    latitude_row = (first_row + row8).astype(F32) + float(NLAT_GLOBE - 64)
    latitude = math.pi * ((latitude_row + 0.5) / NLAT_GLOBE - 0.5)
    metrics[...] = (0.5 / jnp.maximum(jnp.cos(latitude), 0.2))[:, :LANES]

    @pl.loop(0, 8)
    def _(j):
        metric = jnp.broadcast_to(metrics[pl.ds(j, 1), :], (8, LANES))
        beside = field[tile(j * 13 + 12), :]
        for g in range(STEPS):
            if g == STEPS - 1:
                after = jnp.where(
                    row8 == 7, wide(beside[1:2, :]), pltpu.roll(field[tile(j * 13), :], 7, 0)
                )
            else:
                after = field[tile(j * 13 + g + 1), :]
            if g == 0:
                ahead = jnp.where(
                    row8 == 0, wide(beside[0:1, :]), pltpu.roll(field[tile(j * 13 + 11), :], 1, 0)
                )
            else:
                ahead = field[tile(j * 13 + g - 1), :]
            along = after - ahead
            slope = slopes[tile(j * 12 + g), :]
            eastern = along[:, LANES:] * metric - slope[:, :LANES]
            northern = pltpu.roll(along[:, :LANES] * metric + slope[:, LANES:], LANES - 1, 1)
            at = j * COLS + g
            mixed[pl.ds(at, 8, stride=12), :] = jnp.where(lane < NLEV, eastern, northern)
            mixed[pl.ds(768 + at, 8, stride=12), :] = northern

    kept_winds = pltpu.make_async_copy(mixed, winds_ref, in_sem)
    kept_winds.start()

    pltpu.make_async_copy(fifteen, fifteen, lon_sems.at[0]).wait()
    pltpu.make_async_copy(seven, seven, side_sems.at[0]).wait()
    for c in range(count):
        near[c].wait_send()
        far[c].wait_send()
        for d in range(1, 4):

            @pl.when(target_there(d))
            def _():
                chip_copy(c, d).wait_send()

    kept.wait()
    kept_winds.wait()
    others = blocks_out.at[pl.ds(0, 127)]
    landed = arrived_ref.at[pl.ds(0, 127)]
    pltpu.make_async_copy(others, others, all_sems.at[0]).wait()
    pltpu.make_async_copy(landed, landed, all_sems.at[1]).wait()


def slabs_kernel(arrived_ref, low_ref, high_ref, slabs_ref, winds_ref):
    lane = iota((8, LANES), 1)
    block = lane // 32
    for q, g in [(q, g) for q in range(LATS) for g in range(4)]:
        got = [
            [arrived_ref[16 * q + 4 * g + l, :, c * LANES : (c + 1) * LANES] for c in range(3)]
            for l in range(4)
        ]

        def put(slot, v, value):
            at = (g * 3 + v) * LANES
            slabs_ref[slot, 8 * q : 8 * q + 8, at : at + LANES] = value

        moved = []
        for c in range(3):
            for v, width in enumerate((96, 64, 32)):
                put(c, v, jnp.where(lane < width, got[v][c], got[v + 1][c]))
            merged = jnp.where(
                block == 3,
                got[0][c],
                jnp.where(block == 2, got[1][c], jnp.where(block == 1, got[2][c], got[3][c])),
            )
            moved.append(pltpu.roll(merged, 32 * (c + 1), 1))
        for v in range(3):
            parts = [moved[(4 * v + b) % 3] for b in range(4)]
            value = jnp.where(
                block == 0,
                parts[0],
                jnp.where(block == 1, parts[1], jnp.where(block == 2, parts[2], parts[3])),
            )
            put(3, v, value)
    for q in range(LATS):
        winds_ref[q, :, 0:LANES] = low_ref[q * COLS : (q + 1) * COLS, :]
        winds_ref[q, :, LANES : 2 * NLEV] = high_ref[q * COLS : (q + 1) * COLS, 0 : 2 * NLEV - LANES]


def shards(control, vert_band, lat_length, lon_length, band_index, owner_device):
    vmem = pltpu.VMEM
    edge = vmem((HIGH, WIDE), F32)
    dma = pltpu.SemaphoreType.DMA
    count = len(CHUNKS)
    arrived, winds_wide = pl.pallas_call(
        columns_kernel,
        out_shape=(
            jax.ShapeDtypeStruct((128, 8, 3 * LANES), F32),
            jax.ShapeDtypeStruct((16 * COLS, LANES), F32),
        ),
        in_specs=[
            pl.BlockSpec(memory_space=pltpu.SMEM),
        ]
        + [pl.BlockSpec(memory_space=pl.ANY)] * 5,
        out_specs=(pl.BlockSpec(memory_space=pl.ANY), pl.BlockSpec(memory_space=pl.ANY)),
        scratch_shapes=[
            vmem((8, COLS, 2 * NLEV), F32),
            vmem((8, 2 * NLEV), F32),
            vmem((1, 2 * NLEV), F32),
            vmem((9, 2, NLEV), F32),
            vmem((1, 2 * NLEV), jnp.int32),
            vmem((32, WIDE), F32),
            vmem((8 * COLS, WIDE), BF),
            vmem((8 * COLS, WIDE), BF),
            vmem((WIDE, WIDE), BF),
            vmem((WIDE, WIDE), BF),
            vmem((16 * COLS, LANES), F32),
            vmem((8 * HIGH, WIDE), F32),
            vmem((8 * COLS, WIDE), F32),
            vmem((16 * COLS, LANES), F32),
            vmem((8 * LANES, WIDE), BF),
            vmem((8 * LANES, WIDE), BF),
            vmem((512, WIDE), BF),
            vmem((4096, LANES), F32),
            vmem((128, 8, 3 * LANES), F32),
            vmem((8, 1, WIDE), F32),
            vmem((128, LANES), F32),
            vmem((128, LANES), F32),
            vmem((64, WIDE), F32),
            vmem((64, WIDE), F32),
            vmem((32, WIDE), F32),
            vmem((8, LANES), F32),
            vmem((COLS, WIDE), F32),
            vmem((64, WIDE), F32),
            vmem((64, WIDE), F32),
            vmem((16, WIDE), F32),
            vmem((16, 16, WIDE), F32),
            vmem((32, WIDE), F32),
            vmem((64, WIDE), F32),
            vmem((8, WIDE), F32),
            vmem((8, 8, WIDE), F32),
            vmem((80, WIDE), F32),
            vmem((80, WIDE), F32),
            vmem((64, WIDE), F32),
            edge,
            edge,
            edge,
            edge,
            vmem((3, HIGH, WIDE), F32),
            edge,
            edge,
            edge,
            dma,
            dma((4,)),
            dma((2,)),
            dma((2,)),
            dma((2, count)),
            dma((count, 3)),
            dma((count, 3)),
            dma((2, count)),
            dma((3,)),
        ],
        compiler_params=pltpu.CompilerParams(collective_id=0, has_side_effects=True),
        name="columns",
    )(
        band_index,
        lat_length.T,
        lon_length[None, :],
        vert_band.transpose(1, 0, 2),
        owner_device.T,
        control.transpose(1, 2, 0),
    )
    slabs, winds = pl.pallas_call(
        slabs_kernel,
        grid=(8 // LATS,),
        out_shape=(
            jax.ShapeDtypeStruct((SLOTS, 64, 1536), F32),
            jax.ShapeDtypeStruct((8, COLS, 2 * NLEV), F32),
        ),
        in_specs=[
            pl.BlockSpec((16 * LATS, 8, 3 * LANES), lambda i: (i, 0, 0)),
            pl.BlockSpec((COLS * LATS, LANES), lambda i: (i, 0)),
            pl.BlockSpec((COLS * LATS, LANES), lambda i: (8 // LATS + i, 0)),
        ],
        out_specs=(
            pl.BlockSpec((SLOTS, 8 * LATS, 1536), lambda i: (0, i, 0)),
            pl.BlockSpec((LATS, COLS, 2 * NLEV), lambda i: (i, 0, 0)),
        ),
        name="slabs",
    )(arrived, winds_wide, winds_wide)
    return (winds.transpose(2, 0, 1), slabs)


def solution(mesh):
    placed = (P(None, "lat", "lon"), P(), P(), P(), P(), P())
    return jax.shard_map(
        shards,
        mesh=mesh,
        in_specs=placed,
        out_specs=(P(None, "lat", "lon"), P(("lat", "lon"), None, None)),
        check_vma=False,
    )
```
